32 devices in a mesh: dp: 4 (over y, x), tensor: 8 (over z, core).
Axes of the slice: x: 2, y: 2, z: 4, core: 2. Of those that a mesh axis runs over, the one named last changes fastest.
Arguments:
- latents: bfloat16 [4, 2048, 1152], P('dp', 'tensor'), may hold values from -6 to 6
- conditioning: bfloat16 [4, 1152], P('dp', 'tensor'), may hold values from -6 to 6
- ada_weight: bfloat16 [2, 1152, 6912], P(None, 'tensor'), may hold values from -0.1875 to 0.1875
- ada_bias: bfloat16 [2, 6912], replicated, may hold values from -3 to 3
- qkv_weight: bfloat16 [2, 1152, 3, 1152], P(None, None, None, 'tensor'), may hold values from -0.1875 to 0.1875
- qkv_bias: bfloat16 [2, 2, 1152], P(None, None, 'tensor'), may hold values from -3 to 3
- out_weight: bfloat16 [2, 1152, 1152], P(None, 'tensor'), may hold values from -0.75 to 0.75
- out_bias: bfloat16 [2, 1152], replicated, may hold values from -3 to 3
- fc1_weight: bfloat16 [2, 1152, 4608], P(None, None, 'tensor'), may hold values from -0.1875 to 0.1875
- fc1_bias: bfloat16 [2, 4608], P(None, 'tensor'), may hold values from -3 to 3
- fc2_weight: bfloat16 [2, 4608, 1152], P(None, 'tensor'), may hold values from -0.09375 to 0.09375
- fc2_bias: bfloat16 [2, 1152], replicated, may hold values from -3 to 3
- out_grad: bfloat16 [4, 2048, 1152], P('dp', 'tensor'), may hold values from -6 to 6
Outputs:
- layer_output: bfloat16 [4, 2048, 1152], P('dp', 'tensor')
- latents_grad: bfloat16 [4, 2048, 1152], P('dp', 'tensor')
- conditioning_grad: bfloat16 [4, 1152], P('dp', 'tensor')
- ada_weight_grad: float32 [2, 1152, 6912], P(None, 'tensor')
- ada_bias_grad: float32 [2, 6912], replicated
- qkv_weight_grad: float32 [2, 1152, 3, 1152], P(None, None, None, 'tensor')
- qkv_bias_grad: float32 [2, 2, 1152], P(None, None, 'tensor')
- out_weight_grad: float32 [2, 1152, 1152], P(None, 'tensor')
- out_bias_grad: float32 [2, 1152], replicated
- fc1_weight_grad: float32 [2, 1152, 4608], P(None, None, 'tensor')
- fc1_bias_grad: float32 [2, 4608], P(None, 'tensor')
- fc2_weight_grad: float32 [2, 4608, 1152], P(None, 'tensor')
- fc2_bias_grad: float32 [2, 1152], replicated
The draws below stay inside these ranges and needn't reach their ends.
All inputs are finite; a program needn't handle non-finite values.
Results may differ from the reference program's by a relative error of at most 0.04.
Values may be sent and summed in bfloat16 or wider, within the bound.
A program may use at most 256 MiB of HBM per device.

```python
import jax
import jax.numpy as jnp
from jax import lax

D = 1152
HEADS = 16
HEAD_DIM = 72
FF = 4608
PATCHES = 256
FRAMES = 8
LAYERS = 2
TOK = 2048
LATENTS = 4


def levels(key, shape, cuts, low, top_value):
    level = 1.0
    for dim, shards_of in cuts:
        steps = jax.random.uniform(jax.random.fold_in(jax.random.fold_in(key, 6), dim), (shards_of,), jnp.float32, low / len(cuts), top_value / len(cuts))
        level = level * jnp.repeat(jnp.exp(steps), shape[dim] // shards_of).reshape((-1,) + (1,) * (len(shape) - 1 - dim))
    return level


def bell_draw(key, shape, width, bound, pieces=(), dtype=jnp.bfloat16):
    level = levels(key, shape, pieces, -0.22, 0.18) if pieces else 1.0
    values = jax.random.normal(key, shape, jnp.float32) * width * level
    return jnp.minimum(jnp.maximum(values, -bound), bound).astype(dtype)


def setup_inputs(seed: int = 0) -> dict:
    key_list = jax.random.split(jax.random.key(seed), 14)
    return {
        "latents": bell_draw(key_list[0], (LATENTS, TOK, D), 1.0, 6.0, ((0, 4), (1, 8))),
        "conditioning": bell_draw(key_list[1], (LATENTS, D), 1.0, 6.0, ((0, 4), (1, 8))),
        "ada_weight": bell_draw(key_list[2], (LAYERS, D, 6 * D), D ** -0.5, 0.1875, ((1, 8),)),
        "ada_bias": bell_draw(key_list[3], (LAYERS, 6 * D), 0.5, 3.0),
        "qkv_weight": bell_draw(key_list[4], (LAYERS, D, 3, D), D ** -0.5, 0.1875, ((3, 8),)),
        "qkv_bias": bell_draw(key_list[5], (LAYERS, 2, D), 0.5, 3.0, ((2, 8),)),
        "out_weight": bell_draw(key_list[6], (LAYERS, D, D), (D // 16) ** -0.5, 0.75, ((1, 8),)),
        "out_bias": bell_draw(key_list[7], (LAYERS, D), 0.5, 3.0),
        "fc1_weight": bell_draw(key_list[8], (LAYERS, D, FF), D ** -0.5, 0.1875, ((2, 8),)),
        "fc1_bias": bell_draw(key_list[9], (LAYERS, FF), 0.5, 3.0, ((1, 8),)),
        "fc2_weight": bell_draw(key_list[10], (LAYERS, FF, D), FF ** -0.5, 0.09375, ((1, 8),)),
        "fc2_bias": bell_draw(key_list[11], (LAYERS, D), 0.5, 3.0),
        "out_grad": bell_draw(key_list[12], (LATENTS, TOK, D), 1.0, 6.0, ((0, 4), (1, 8))),
    }


@jax.custom_vjp
def low(v):
    return lax.optimization_barrier(v.astype(jnp.bfloat16)).astype(jnp.float32)

@jax.custom_vjp
def low_back(v):
    return v

def low_keep(v):
    return (low(v), None)

def low_pass(kept, grad):
    return (grad,)

def back_keep(v):
    return (v, None)

def back_low(kept, grad):
    return (low(grad),)
low.defvjp(low_keep, low_pass)
low_back.defvjp(back_keep, back_low)

def matmul(left, right):
    return jnp.dot(left, right, precision=lax.Precision.HIGHEST)

def normalize(stream):
    centered = stream - lax.optimization_barrier(jnp.mean(stream, axis=-1, keepdims=True))
    variance = lax.optimization_barrier(jnp.mean(centered * centered, axis=-1, keepdims=True))
    return centered * lax.rsqrt(variance + 1e-06)

def grouped(token_rows, spatial):
    shaped = token_rows.reshape(FRAMES, PATCHES, HEADS, HEAD_DIM)
    if spatial:
        return shaped
    return jnp.transpose(shaped, (1, 0, 2, 3))

def ungrouped(groups, spatial):
    if not spatial:
        groups = jnp.transpose(groups, (1, 0, 2, 3))
    return groups.reshape(FRAMES * PATCHES, HEADS * HEAD_DIM)

def attend(query_rows, key_rows, value_rows, spatial):
    query_g = grouped(query_rows, spatial)
    key_g = grouped(key_rows, spatial)
    value_g = grouped(value_rows, spatial)
    scores = jnp.einsum('gqhd,gkhd->ghqk', query_g, key_g, precision=lax.Precision.HIGHEST) * HEAD_DIM ** (-0.5)
    scores = low_back(scores)
    attn_probs = low(jax.nn.softmax(scores, axis=-1))
    mixed = jnp.einsum('ghqk,gkhd->gqhd', attn_probs, value_g, precision=lax.Precision.HIGHEST)
    return ungrouped(mixed, spatial)

def block(stream, silu_cond, params, spatial):
    ada_w, ada_b, qkv_w, qkv_b, out_w, out_b, fc1_w, fc1_b, fc2_w, fc2_b = params
    modulation = low_back(matmul(silu_cond, ada_w) + ada_b)
    shift_att, scale_att, gate_att, shift_mlp, scale_mlp, gate_mlp = jnp.split(modulation, 6)
    normed = low(normalize(stream) * (1.0 + scale_att) + shift_att)
    proj_width = HEADS * HEAD_DIM
    projected = matmul(normed, qkv_w.reshape(D, 3 * proj_width))
    query_rows = low_back(low(projected[:, :proj_width] + qkv_b[0]))
    key_rows = low_back(low(projected[:, proj_width:2 * proj_width]))
    value_rows = low_back(low(projected[:, 2 * proj_width:] + qkv_b[1]))
    heads_out = low_back(low(attend(query_rows, key_rows, value_rows, spatial)))
    attn_branch = low_back(matmul(heads_out, out_w) + out_b)
    middle = stream + gate_att * attn_branch
    normed_mlp = low(normalize(middle) * (1.0 + scale_mlp) + shift_mlp)
    hidden = low_back(matmul(normed_mlp, fc1_w) + fc1_b)
    activated = low(jax.nn.gelu(hidden, approximate=True))
    mlp_branch = low_back(matmul(activated, fc2_w) + fc2_b)
    return middle + gate_mlp * mlp_branch

def forward(latents, conditioning, ada_weight, ada_bias, qkv_weight, qkv_bias, out_weight, out_bias, fc1_weight, fc1_bias, fc2_weight, fc2_bias):
    stacked = (ada_weight, ada_bias, qkv_weight, qkv_bias, out_weight, out_bias, fc1_weight, fc1_bias, fc2_weight, fc2_bias)

    def one_latent(unused_carry, latent_item):
        stream, cond_row = latent_item
        silu_cond = low(jax.nn.silu(cond_row))
        for layer_idx in range(LAYERS):
            params = tuple((member[layer_idx] for member in stacked))
            stream = block(stream, silu_cond, params, layer_idx % 2 == 0)
        return (unused_carry, stream)
    start = jnp.zeros((), jnp.float32)
    _, result = lax.scan(jax.checkpoint(one_latent), start, (latents, conditioning))
    return result

def reference(latents, conditioning, ada_weight, ada_bias, qkv_weight, qkv_bias, out_weight, out_bias, fc1_weight, fc1_bias, fc2_weight, fc2_bias, out_grad):
    inputs = tuple((member.astype(jnp.float32) for member in (latents, conditioning, ada_weight, ada_bias, qkv_weight, qkv_bias, out_weight, out_bias, fc1_weight, fc1_bias, fc2_weight, fc2_bias)))
    result, pullback = jax.vjp(forward, *inputs)
    grads = pullback(out_grad.astype(jnp.float32))
    return (result.astype(jnp.bfloat16), grads[0].astype(jnp.bfloat16), grads[1].astype(jnp.bfloat16), grads[2], grads[3], grads[4], grads[5], grads[6], grads[7], grads[8], grads[9], grads[10], grads[11])
```

```python
from functools import partial

import jax
import jax.numpy as jnp
from jax import lax
from jax.sharding import Mesh, PartitionSpec as P

HEAD_DIM = 72
PATCHES = 256
FRAMES = 8
LAYERS = 2


def normalize(stream):
    centered = stream - jnp.mean(stream, axis=-1, keepdims=True)
    variance = jnp.mean(centered * centered, axis=-1, keepdims=True)
    return centered * lax.rsqrt(variance + 1e-06)


def modulate(stream, shift_in, scale_in):
    return normalize(stream) * (1.0 + scale_in) + shift_in


def grouped(token_rows, spatial):
    heads_here = token_rows.shape[1] // HEAD_DIM
    shaped = token_rows.reshape(FRAMES, PATCHES, heads_here, HEAD_DIM)
    if spatial:
        return shaped
    return jnp.transpose(shaped, (1, 0, 2, 3))


def ungrouped(groups, spatial):
    if not spatial:
        groups = jnp.transpose(groups, (1, 0, 2, 3))
    return groups.reshape(FRAMES * PATCHES, groups.shape[2] * HEAD_DIM)


def softmax_rows(query_g, key_g):
    scores = jnp.einsum(
        "gqhd,gkhd->ghqk", query_g, key_g, preferred_element_type=jnp.float32
    ) * HEAD_DIM ** (-0.5)
    return jax.nn.softmax(scores, axis=-1)


def attend(query_rows, key_rows, value_rows, spatial):
    attn_probs = softmax_rows(grouped(query_rows, spatial), grouped(key_rows, spatial)).astype(
        jnp.bfloat16
    )
    mixed = jnp.einsum(
        "ghqk,gkhd->gqhd",
        attn_probs,
        grouped(value_rows, spatial),
        preferred_element_type=jnp.float32,
    )
    return ungrouped(mixed, spatial)


def attend_back(query_rows, key_rows, value_rows, mixed_grad, spatial):
    query_g = grouped(query_rows, spatial)
    key_g = grouped(key_rows, spatial)
    value_g = grouped(value_rows, spatial)
    grad_g = grouped(mixed_grad, spatial)
    probs_full = softmax_rows(query_g, key_g)
    value_grad = jnp.einsum(
        "ghqk,gqhd->gkhd",
        probs_full.astype(jnp.bfloat16),
        grad_g,
        preferred_element_type=jnp.float32,
    )
    probs_grad = jnp.einsum("gqhd,gkhd->ghqk", grad_g, value_g, preferred_element_type=jnp.float32)
    score_grad = probs_full * (
        probs_grad - jnp.sum(probs_grad * probs_full, axis=-1, keepdims=True)
    )
    score_low = score_grad.astype(jnp.bfloat16)
    factor = HEAD_DIM ** (-0.5)
    query_grad = (
        jnp.einsum("ghqk,gkhd->gqhd", score_low, key_g, preferred_element_type=jnp.float32) * factor
    )
    key_grad = (
        jnp.einsum("ghqk,gqhd->gkhd", score_low, query_g, preferred_element_type=jnp.float32)
        * factor
    )
    return (
        ungrouped(query_grad, spatial),
        ungrouped(key_grad, spatial),
        ungrouped(value_grad, spatial),
    )


def spread_rows(row_block):
    return lax.all_gather(row_block, "tensor", axis=0, tiled=True)


def reduce_rows(partial_terms):
    return lax.psum_scatter(
        partial_terms.astype(jnp.bfloat16), "tensor", scatter_dimension=0, tiled=True
    ).astype(jnp.float32)


def spread_grads(row_block):
    return lax.all_gather(row_block, "tensor", axis=0, tiled=True)


def reduce_grads(partial_terms):
    return lax.psum_scatter(
        partial_terms.astype(jnp.bfloat16), "tensor", scatter_dimension=0, tiled=True
    ).astype(jnp.float32)


def layer_forward(stream, modulation, params, spatial):
    qkv_w, qkv_b, out_w, out_b, fc1_w, fc1_b, fc2_w, fc2_b = params
    shift_att, scale_att, gate_att, shift_mlp, scale_mlp, gate_mlp = jnp.split(modulation, 6)
    normed = spread_rows(modulate(stream, shift_att, scale_att).astype(jnp.bfloat16))
    head_width = qkv_w.shape[2]
    projected = jnp.dot(
        normed, qkv_w.reshape(qkv_w.shape[0], 3 * head_width), preferred_element_type=jnp.float32
    )
    query_rows = (projected[:, :head_width] + qkv_b[0].astype(jnp.float32)).astype(jnp.bfloat16)
    key_rows = projected[:, head_width : 2 * head_width].astype(jnp.bfloat16)
    value_rows = (projected[:, 2 * head_width :] + qkv_b[1].astype(jnp.float32)).astype(
        jnp.bfloat16
    )
    heads_out = attend(query_rows, key_rows, value_rows, spatial).astype(jnp.bfloat16)
    attn_branch = reduce_rows(
        jnp.dot(heads_out, out_w, preferred_element_type=jnp.float32)
    ) + out_b.astype(jnp.float32)
    middle = stream + gate_att * attn_branch
    normed_mlp = spread_rows(modulate(middle, shift_mlp, scale_mlp).astype(jnp.bfloat16))
    hidden = jnp.dot(normed_mlp, fc1_w, preferred_element_type=jnp.float32) + fc1_b.astype(
        jnp.float32
    )
    activated = jax.nn.gelu(hidden, approximate=True).astype(jnp.bfloat16)
    mlp_branch = reduce_rows(
        jnp.dot(activated, fc2_w, preferred_element_type=jnp.float32)
    ) + fc2_b.astype(jnp.float32)
    result = middle + gate_mlp * mlp_branch
    saved = (
        normed,
        query_rows,
        key_rows,
        value_rows,
        heads_out,
        attn_branch,
        middle,
        normed_mlp,
        hidden,
        mlp_branch,
    )
    return (result, saved)


def layer_backward(stream, modulation, params, saved, stream_grad, spatial):
    qkv_w, qkv_b, out_w, out_b, fc1_w, fc1_b, fc2_w, fc2_b = params
    (
        normed,
        query_rows,
        key_rows,
        value_rows,
        heads_out,
        attn_branch,
        middle,
        normed_mlp,
        hidden,
        mlp_branch,
    ) = saved
    shift_att, scale_att, gate_att, shift_mlp, scale_mlp, gate_mlp = jnp.split(modulation, 6)
    head_width = qkv_w.shape[2]
    mlp_grad = (gate_mlp * stream_grad).astype(jnp.bfloat16)
    gate_mlp_grad = jnp.sum(stream_grad * mlp_branch, axis=0)
    fc2_b_grad = jnp.sum(mlp_grad, axis=0, dtype=jnp.float32)
    mlp_grad_all = spread_grads(mlp_grad)
    gelu_out, gelu_back = jax.vjp(partial(jax.nn.gelu, approximate=True), hidden)
    activated = gelu_out.astype(jnp.bfloat16)
    fc2_w_grad = jnp.einsum(
        "tf,td->fd", activated, mlp_grad_all, preferred_element_type=jnp.float32
    )
    act_grad = jnp.einsum("td,fd->tf", mlp_grad_all, fc2_w, preferred_element_type=jnp.float32)
    hidden_grad = gelu_back(act_grad)[0].astype(jnp.bfloat16)
    fc1_b_grad = jnp.sum(hidden_grad, axis=0, dtype=jnp.float32)
    fc1_w_grad = jnp.einsum(
        "td,tf->df", normed_mlp, hidden_grad, preferred_element_type=jnp.float32
    )
    mlp_in_grad = reduce_grads(
        jnp.einsum("tf,df->td", hidden_grad, fc1_w, preferred_element_type=jnp.float32)
    )
    _, mlp_norm_back = jax.vjp(modulate, middle, shift_mlp, scale_mlp)
    middle_part, shift_mlp_grad, scale_mlp_grad = mlp_norm_back(mlp_in_grad)
    middle_grad = stream_grad + middle_part
    attn_grad = (gate_att * middle_grad).astype(jnp.bfloat16)
    gate_att_grad = jnp.sum(middle_grad * attn_branch, axis=0)
    out_b_grad = jnp.sum(attn_grad, axis=0, dtype=jnp.float32)
    attn_grad_all = spread_grads(attn_grad)
    out_w_grad = jnp.einsum(
        "tw,td->wd", heads_out, attn_grad_all, preferred_element_type=jnp.float32
    )
    heads_grad = jnp.einsum(
        "td,wd->tw", attn_grad_all, out_w, preferred_element_type=jnp.float32
    ).astype(jnp.bfloat16)
    query_grad, key_grad, value_grad = attend_back(
        query_rows, key_rows, value_rows, heads_grad, spatial
    )
    qkv_grad = jnp.concatenate([query_grad, key_grad, value_grad], axis=1).astype(jnp.bfloat16)
    qkv_b_grad = jnp.stack(
        [
            jnp.sum(qkv_grad[:, :head_width], axis=0, dtype=jnp.float32),
            jnp.sum(qkv_grad[:, 2 * head_width :], axis=0, dtype=jnp.float32),
        ]
    )
    qkv_flat = qkv_w.reshape(qkv_w.shape[0], 3 * head_width)
    qkv_w_grad = jnp.einsum(
        "td,tw->dw", normed, qkv_grad, preferred_element_type=jnp.float32
    ).reshape(qkv_w.shape)
    attn_in_grad = reduce_grads(
        jnp.einsum("tw,dw->td", qkv_grad, qkv_flat, preferred_element_type=jnp.float32)
    )
    _, att_norm_back = jax.vjp(modulate, stream, shift_att, scale_att)
    stream_part, shift_att_grad, scale_att_grad = att_norm_back(attn_in_grad)
    input_grad = middle_grad + stream_part
    modulation_grad = jnp.concatenate(
        [
            shift_att_grad,
            scale_att_grad,
            gate_att_grad,
            shift_mlp_grad,
            scale_mlp_grad,
            gate_mlp_grad,
        ]
    )
    return (
        input_grad,
        modulation_grad,
        (
            qkv_w_grad,
            qkv_b_grad,
            out_w_grad,
            out_b_grad,
            fc1_w_grad,
            fc1_b_grad,
            fc2_w_grad,
            fc2_b_grad,
        ),
    )


def per_device(
    latents,
    conditioning,
    ada_weight,
    ada_bias,
    qkv_weight,
    qkv_bias,
    out_weight,
    out_bias,
    fc1_weight,
    fc1_bias,
    fc2_weight,
    fc2_bias,
    out_grad,
):
    cond_row = conditioning[0].astype(jnp.float32)
    silu_out, silu_back = jax.vjp(jax.nn.silu, cond_row)
    silu_cond = silu_out.astype(jnp.bfloat16)
    ada_terms = jnp.einsum("d,ldm->lm", silu_cond, ada_weight, preferred_element_type=jnp.float32)
    modulations = lax.psum(ada_terms, "tensor") + ada_bias.astype(jnp.float32)
    stacked = (
        qkv_weight,
        qkv_bias,
        out_weight,
        out_bias,
        fc1_weight,
        fc1_bias,
        fc2_weight,
        fc2_bias,
    )
    stream = latents[0].astype(jnp.float32)
    inputs_kept = []
    saved_all = []
    for layer_idx in range(LAYERS):
        params = tuple((member[layer_idx] for member in stacked))
        inputs_kept.append(stream)
        stream, saved = layer_forward(stream, modulations[layer_idx], params, layer_idx % 2 == 0)
        saved_all.append(saved)
    layer_output = stream.astype(jnp.bfloat16)[None]
    stream_grad = out_grad[0].astype(jnp.float32)
    mod_grads = [None] * LAYERS
    layer_grads = [None] * LAYERS
    for layer_idx in reversed(range(LAYERS)):
        params = tuple((member[layer_idx] for member in stacked))
        spatial = layer_idx % 2 == 0
        saved = layer_forward(inputs_kept[layer_idx], modulations[layer_idx], params, spatial)[1]
        stream_grad, mod_grads[layer_idx], layer_grads[layer_idx] = layer_backward(
            inputs_kept[layer_idx], modulations[layer_idx], params, saved, stream_grad, spatial
        )

    def collect(position):
        return jnp.stack([member[position] for member in layer_grads])

    mod_sum, out_b_sum, fc2_b_sum = (
        lax.psum(jnp.stack(mod_grads).astype(jnp.bfloat16), "tensor").astype(jnp.float32),
        lax.psum(collect(3).astype(jnp.bfloat16), "tensor").astype(jnp.float32),
        lax.psum(collect(7).astype(jnp.bfloat16), "tensor").astype(jnp.float32),
    )
    mod_low = mod_sum.astype(jnp.bfloat16)
    ada_w_grad = (
        silu_cond.astype(jnp.float32)[None, :, None] * mod_low.astype(jnp.float32)[:, None, :]
    )
    ada_b_grad = mod_low.astype(jnp.float32)
    silu_grad = jnp.einsum("lm,ldm->d", mod_low, ada_weight, preferred_element_type=jnp.float32)
    cond_grad = silu_back(silu_grad)[0]
    summed = (
        lax.psum(ada_w_grad.astype(jnp.bfloat16), "dp").astype(jnp.float32),
        lax.psum(ada_b_grad.astype(jnp.bfloat16), "dp").astype(jnp.float32),
        lax.psum(collect(0).astype(jnp.bfloat16), "dp").astype(jnp.float32),
        lax.psum(collect(1).astype(jnp.bfloat16), "dp").astype(jnp.float32),
        lax.psum(collect(2).astype(jnp.bfloat16), "dp").astype(jnp.float32),
        lax.psum(out_b_sum.astype(jnp.bfloat16), "dp").astype(jnp.float32),
        lax.psum(collect(4).astype(jnp.bfloat16), "dp").astype(jnp.float32),
        lax.psum(collect(5).astype(jnp.bfloat16), "dp").astype(jnp.float32),
        lax.psum(collect(6).astype(jnp.bfloat16), "dp").astype(jnp.float32),
        lax.psum(fc2_b_sum.astype(jnp.bfloat16), "dp").astype(jnp.float32),
    )
    return (
        layer_output,
        stream_grad.astype(jnp.bfloat16)[None],
        cond_grad.astype(jnp.bfloat16)[None],
        summed[0],
        summed[1],
        summed[2],
        summed[3],
        summed[4],
        summed[5],
        summed[6],
        summed[7],
        summed[8],
        summed[9],
    )


LINE = ("z", "c")
PLANE = ("y", "x")


def swap(value, axis):
    return lax.ppermute(value, axis, [(0, 1), (1, 0)])


def pick(value, index, axis=0):
    return lax.dynamic_index_in_dim(value, index, axis, keepdims=False)


def gather_attention(qkv_w, out_w):
    me_c = lax.axis_index("c")
    me = 2 * lax.axis_index("y") + lax.axis_index("x")
    mine = pick(jnp.concatenate([jnp.transpose(qkv_w, (1, 2, 0)), out_w[None]]), me)
    whole = lax.all_gather(mine, LINE, axis=0).reshape((4, 2) + mine.shape)
    half = pick(whole, me_c, 1)
    from_x = swap(half, "x")
    from_y = swap(half, "y")
    from_xy = swap(from_x, "y")
    result = jnp.zeros((4,) + whole.shape, whole.dtype)
    result = lax.dynamic_update_slice(result, whole[None], (me, 0, 0, 0, 0))
    for flip, part in ((1, from_x), (2, from_y), (3, from_xy)):
        other = swap(part, "c")
        result = lax.dynamic_update_slice(
            result, part[None, :, None], (me ^ flip, 0, me_c, 0, 0)
        )
        result = lax.dynamic_update_slice(
            result, other[None, :, None], (me ^ flip, 0, 1 - me_c, 0, 0)
        )
    return result


def gather_hidden(piece):
    me_c = lax.axis_index("c")
    whole = lax.all_gather(piece, LINE, axis=0).reshape((4, 2) + piece.shape)
    part = swap(pick(whole, me_c, 1), "y")
    other = swap(part, "c")
    width = piece.shape[-1]
    return jnp.concatenate(
        [whole.reshape(-1, width), part.reshape(-1, width), other.reshape(-1, width)]
    )


def hidden_order(quarters):
    me_c = lax.axis_index("c")
    me = 2 * lax.axis_index("y") + lax.axis_index("x")
    near = pick(quarters, me ^ 2, 2)
    return jnp.concatenate(
        [
            pick(quarters, me, 2).reshape(-1),
            pick(near, me_c, 1).reshape(-1),
            pick(near, 1 - me_c, 1).reshape(-1),
        ]
    )


def hidden_place(values):
    me_c = lax.axis_index("c")
    me = 2 * lax.axis_index("y") + lax.axis_index("x")
    count = values.shape[0] // 16
    own = values[: 8 * count].reshape(4, 2, 1, count)
    part = values[8 * count : 12 * count].reshape(4, 1, 1, count)
    other = values[12 * count :].reshape(4, 1, 1, count)
    result = jnp.zeros((4, 2, 4, count), values.dtype)
    result = lax.dynamic_update_slice(result, own, (0, 0, me, 0))
    result = lax.dynamic_update_slice(result, part, (0, me_c, me ^ 2, 0))
    return lax.dynamic_update_slice(result, other, (0, 1 - me_c, me ^ 2, 0))


def reduce_line(blocks):
    mine = lax.psum_scatter(blocks, "z", scatter_dimension=0, tiled=False)
    return lax.all_gather(mine, PLANE, axis=0)


def reduce_attention(grads):
    me_c, me_x, me_y = lax.axis_index("c"), lax.axis_index("x"), lax.axis_index("y")
    low = jnp.bfloat16
    kept = pick(grads, me_c, 2) + swap(pick(grads, 1 - me_c, 2), "c")
    kept = kept.reshape((2, 2) + kept.shape[1:])
    kept = pick(kept, me_y) + swap(pick(kept, 1 - me_y), "y")
    kept = pick(kept, me_x) + swap(pick(kept, 1 - me_x), "x")
    return reduce_line(kept.astype(low))


def reduce_hidden(grads):
    me_c = lax.axis_index("c")
    rows, width = grads.shape[0] // 16, grads.shape[1]
    own = grads[: 8 * rows].reshape(4, 2, rows, width)
    part = grads[8 * rows : 12 * rows].reshape(4, rows, width)
    other = grads[12 * rows :].reshape(4, rows, width)
    part = part + swap(other, "c")
    own = pick(own, me_c, 1) + swap(pick(own, 1 - me_c, 1), "c")
    return reduce_line(own + swap(part, "y")).reshape(4 * rows, width)


def to_heads(rows):
    return rows.reshape(rows.shape[0], -1, HEAD_DIM)


def local_probs(query, key, mask):
    scores = jnp.einsum(
        "qhd,khd->hqk", to_heads(query), to_heads(key), preferred_element_type=jnp.float32
    ) * HEAD_DIM ** (-0.5)
    if mask is not None:
        scores = jnp.where(mask, scores, -jnp.inf)
    return jax.nn.softmax(scores, axis=-1)


def local_attend(query, key, value, mask):
    probs = local_probs(query, key, mask).astype(jnp.bfloat16)
    mixed = jnp.einsum("hqk,khd->qhd", probs, to_heads(value), preferred_element_type=jnp.float32)
    return mixed.reshape(query.shape).astype(jnp.bfloat16)


def local_attend_back(query, key, value, grad, mask):
    probs = local_probs(query, key, mask)
    value_grad = jnp.einsum(
        "hqk,qhd->khd",
        probs.astype(jnp.bfloat16),
        to_heads(grad),
        preferred_element_type=jnp.float32,
    )
    probs_grad = jnp.einsum(
        "qhd,khd->hqk", to_heads(grad), to_heads(value), preferred_element_type=jnp.float32
    )
    score_grad = probs * (probs_grad - jnp.sum(probs_grad * probs, axis=-1, keepdims=True))
    score_low = score_grad.astype(jnp.bfloat16)
    factor = HEAD_DIM ** (-0.5)
    query_grad = (
        jnp.einsum("hqk,khd->qhd", score_low, to_heads(key), preferred_element_type=jnp.float32)
        * factor
    )
    key_grad = (
        jnp.einsum("hqk,qhd->khd", score_low, to_heads(query), preferred_element_type=jnp.float32)
        * factor
    )
    return tuple(
        part.reshape(query.shape).astype(jnp.bfloat16)
        for part in (query_grad, key_grad, value_grad)
    )


def rows_dot(left, right):
    return jnp.einsum("tk,rk->tr", left, right, preferred_element_type=jnp.float32)


def weight_grad(left, right):
    return jnp.einsum("tr,td->rd", left, right, preferred_element_type=jnp.float32).astype(
        jnp.bfloat16
    )


def block_forward(stream, modulation, weights, biases, mask):
    qkvo, fc1, fc2 = weights
    query_b, value_b, out_b, fc1_b, fc2_b = biases
    shift_att, scale_att, gate_att, shift_mlp, scale_mlp, gate_mlp = jnp.split(modulation, 6)
    width = stream.shape[1]
    matrices = qkvo.reshape(4 * width, width)
    normed = modulate(stream, shift_att, scale_att).astype(jnp.bfloat16)
    projected = rows_dot(normed, matrices[: 3 * width])
    query = (projected[:, :width] + query_b).astype(jnp.bfloat16)
    key = projected[:, width : 2 * width].astype(jnp.bfloat16)
    value = (projected[:, 2 * width :] + value_b).astype(jnp.bfloat16)
    heads_out = local_attend(query, key, value, mask)
    attn_branch = (
        jnp.dot(heads_out, matrices[3 * width :], preferred_element_type=jnp.float32) + out_b
    )
    middle = stream + gate_att * attn_branch
    normed_mlp = modulate(middle, shift_mlp, scale_mlp).astype(jnp.bfloat16)
    both = (normed_mlp, swap(normed_mlp, "x"))
    hidden = [rows_dot(part, fc1) + fc1_b for part in both]
    activated = [jax.nn.gelu(part, approximate=True).astype(jnp.bfloat16) for part in hidden]
    terms = [jnp.dot(part, fc2, preferred_element_type=jnp.float32) for part in activated]
    mlp_branch = terms[0] + swap(terms[1].astype(jnp.bfloat16), "x").astype(jnp.float32) + fc2_b
    result = middle + gate_mlp * mlp_branch
    saved = (
        normed,
        query,
        key,
        value,
        heads_out,
        attn_branch,
        middle,
        both,
        hidden,
        activated,
        mlp_branch,
    )
    return result, saved


def block_backward(stream, modulation, weights, saved, stream_grad, mask):
    qkvo, fc1, fc2 = weights
    (
        normed,
        query,
        key,
        value,
        heads_out,
        attn_branch,
        middle,
        both,
        hidden,
        activated,
        mlp_branch,
    ) = saved
    shift_att, scale_att, gate_att, shift_mlp, scale_mlp, gate_mlp = jnp.split(modulation, 6)
    width = stream.shape[1]
    matrices = qkvo.reshape(4 * width, width)
    mlp_grad = (gate_mlp * stream_grad).astype(jnp.bfloat16)
    gate_mlp_grad = jnp.sum(stream_grad * mlp_branch, axis=0)
    fc2_b_grad = jnp.sum(mlp_grad, axis=0, dtype=jnp.float32)
    mlp_grads = (mlp_grad, swap(mlp_grad, "x"))
    hidden_grads = []
    for part, grad in zip(hidden, mlp_grads):
        _, gelu_back = jax.vjp(partial(jax.nn.gelu, approximate=True), part)
        hidden_grads.append(gelu_back(rows_dot(grad, fc2))[0].astype(jnp.bfloat16))
    terms = [jnp.dot(part, fc1, preferred_element_type=jnp.float32) for part in hidden_grads]
    mlp_in_grad = terms[0] + swap(terms[1].astype(jnp.bfloat16), "x").astype(jnp.float32)
    hidden_grad = jnp.concatenate(hidden_grads)
    fc1_b_grad = jnp.sum(hidden_grad, axis=0, dtype=jnp.float32)
    fc2_grad = weight_grad(jnp.concatenate(activated), jnp.concatenate(mlp_grads))
    fc1_grad = weight_grad(hidden_grad, jnp.concatenate(both))
    _, mlp_norm_back = jax.vjp(modulate, middle, shift_mlp, scale_mlp)
    middle_part, shift_mlp_grad, scale_mlp_grad = mlp_norm_back(mlp_in_grad)
    middle_grad = stream_grad + middle_part
    attn_grad = (gate_att * middle_grad).astype(jnp.bfloat16)
    gate_att_grad = jnp.sum(middle_grad * attn_branch, axis=0)
    out_b_grad = jnp.sum(attn_grad, axis=0, dtype=jnp.float32)
    out_grad = weight_grad(heads_out, attn_grad)
    heads_grad = rows_dot(attn_grad, matrices[3 * width :]).astype(jnp.bfloat16)
    qkv_grads = local_attend_back(query, key, value, heads_grad, mask)
    qkv_grad = jnp.concatenate(qkv_grads, axis=1)
    qkv_w_grad = weight_grad(qkv_grad, normed)
    qkvo_grad = jnp.concatenate([qkv_w_grad, out_grad]).reshape(qkvo.shape)
    attn_in_grad = jnp.dot(qkv_grad, matrices[: 3 * width], preferred_element_type=jnp.float32)
    _, att_norm_back = jax.vjp(modulate, stream, shift_att, scale_att)
    stream_part, shift_att_grad, scale_att_grad = att_norm_back(attn_in_grad)
    input_grad = middle_grad + stream_part
    small = jnp.concatenate(
        [
            shift_att_grad,
            scale_att_grad,
            gate_att_grad,
            shift_mlp_grad,
            scale_mlp_grad,
            gate_mlp_grad,
            jnp.sum(qkv_grads[0], axis=0, dtype=jnp.float32),
            jnp.sum(qkv_grads[2], axis=0, dtype=jnp.float32),
            out_b_grad,
            fc2_b_grad,
            hidden_place(fc1_b_grad).reshape(-1),
        ]
    )
    small = lax.all_gather(lax.psum(small, LINE), PLANE, axis=0)
    return (
        input_grad,
        small,
        reduce_attention(qkvo_grad),
        reduce_hidden(fc1_grad),
        reduce_hidden(fc2_grad),
    )


def frame_parallel(
    latents,
    conditioning,
    ada_weight,
    ada_bias,
    qkv_weight,
    qkv_bias,
    out_weight,
    out_bias,
    fc1_weight,
    fc1_bias,
    fc2_weight,
    fc2_bias,
    out_grad,
):
    me = 2 * lax.axis_index("y") + lax.axis_index("x")
    block = 2 * lax.axis_index("z") + lax.axis_index("c")
    width = latents.shape[2]
    tokens = latents.shape[1]

    def reshard(value):
        return lax.all_to_all(value, LINE, 0, 0, tiled=True)

    silu_out, silu_back = jax.vjp(jax.nn.silu, conditioning[0].astype(jnp.float32))
    silu_cond = silu_out.astype(jnp.bfloat16)
    ada_terms = jnp.einsum("d,ldm->lm", silu_cond, ada_weight, preferred_element_type=jnp.float32)
    modulations = lax.psum(ada_terms, LINE) + ada_bias.astype(jnp.float32)

    quarter = fc1_bias.shape[1] // 4
    weights = []
    for layer in range(LAYERS):
        fc1_rows = jnp.transpose(
            lax.dynamic_slice_in_dim(fc1_weight[layer], me * quarter, quarter, 1)
        )
        fc2_rows = lax.dynamic_slice_in_dim(fc2_weight[layer], me * quarter, quarter, 0)
        weights.append(
            (
                gather_attention(qkv_weight[layer], out_weight[layer]),
                gather_hidden(fc1_rows),
                gather_hidden(fc2_rows),
            )
        )
    head_width = qkv_bias.shape[2]
    small = jnp.concatenate([qkv_bias.reshape(LAYERS, -1), fc1_bias], axis=1)
    small = lax.all_gather(small, LINE, axis=0).astype(jnp.float32)
    biases = []
    for layer in range(LAYERS):
        part = small[:, layer]
        biases.append(
            (
                part[:, :head_width].reshape(-1),
                part[:, head_width : 2 * head_width].reshape(-1),
                out_bias[layer].astype(jnp.float32),
                hidden_order(part[:, 2 * head_width :].reshape(4, 2, 4, quarter)),
                fc2_bias[layer].astype(jnp.float32),
            )
        )

    patch = jnp.arange(tokens) % (PATCHES // 8)
    masks = [None, patch[:, None] == patch[None, :]]
    stream = latents[0].astype(jnp.float32)
    inputs_kept, saved_all = [], []
    for layer in range(LAYERS):
        if layer:
            stream = reshard(stream.astype(jnp.bfloat16)).astype(jnp.float32)
        inputs_kept.append(stream)
        stream, saved = block_forward(
            stream, modulations[layer], weights[layer], biases[layer], masks[layer]
        )
        saved_all.append(saved)
    layer_output = reshard(stream.astype(jnp.bfloat16))[None]

    stream_grad = reshard(out_grad[0]).astype(jnp.float32)
    results = [None] * LAYERS
    for layer in reversed(range(LAYERS)):
        stream_grad, *results[layer] = block_backward(
            inputs_kept[layer],
            modulations[layer],
            weights[layer],
            saved_all[layer],
            stream_grad,
            masks[layer],
        )
        if layer:
            stream_grad = reshard(stream_grad.astype(jnp.bfloat16)).astype(jnp.float32)

    smalls = jnp.stack([member[0] for member in results])
    mod_all = smalls[:, :, : 6 * width].astype(jnp.bfloat16)
    sums = jnp.sum(smalls[:, :, 6 * width :], axis=1)
    silu_all = lax.all_gather(silu_cond, PLANE, axis=0)
    ada_w_grad = jnp.einsum("bk,lbm->lkm", silu_all, mod_all, preferred_element_type=jnp.float32)
    ada_b_grad = jnp.sum(mod_all.astype(jnp.float32), axis=1)
    silu_grad = jnp.einsum(
        "lm,ldm->d", pick(mod_all, me, 1), ada_weight, preferred_element_type=jnp.float32
    )
    cond_grad = silu_back(silu_grad)[0]
    qkv_b_grad = pick(sums[:, : 2 * width].reshape(LAYERS, 2, 8, head_width), block, 2)
    fc1_b_grad = pick(sums[:, 4 * width :].reshape(LAYERS, 8, 4 * quarter), block, 1)
    attention = jnp.stack([member[1] for member in results]).astype(jnp.float32)
    return (
        layer_output,
        stream_grad.astype(jnp.bfloat16)[None],
        cond_grad.astype(jnp.bfloat16)[None],
        ada_w_grad,
        ada_b_grad,
        jnp.transpose(attention[:, :3], (0, 3, 1, 2)),
        qkv_b_grad,
        attention[:, 3],
        sums[:, 2 * width : 3 * width],
        jnp.transpose(
            jnp.stack([member[2] for member in results]).astype(jnp.float32), (0, 2, 1)
        ),
        fc1_b_grad,
        jnp.stack([member[3] for member in results]).astype(jnp.float32),
        sums[:, 3 * width : 4 * width],
    )


def solution(mesh):
    dp, tensor = mesh.shape["dp"], mesh.shape["tensor"]
    if dp == 4 and tensor == 8:
        split = Mesh(mesh.devices.reshape(2, 2, 4, 2), ("y", "x", "z", "c"))
        return sharded(split, frame_parallel, ("y", "x"), ("z", "c"))
    return sharded(mesh, per_device, "dp", "tensor")


def sharded(mesh, body, dp, tensor):
    in_specs = (
        P(dp, tensor, None),
        P(dp, tensor),
        P(None, tensor, None),
        P(),
        P(None, None, None, tensor),
        P(None, None, tensor),
        P(None, tensor, None),
        P(),
        P(None, None, tensor),
        P(None, tensor),
        P(None, tensor, None),
        P(),
        P(dp, tensor, None),
    )
    out_specs = (
        P(dp, tensor, None),
        P(dp, tensor, None),
        P(dp, tensor),
        P(None, tensor, None),
        P(),
        P(None, None, None, tensor),
        P(None, None, tensor),
        P(None, tensor, None),
        P(),
        P(None, None, tensor),
        P(None, tensor),
        P(None, tensor, None),
        P(),
    )
    return jax.shard_map(body, mesh=mesh, in_specs=in_specs, out_specs=out_specs, check_vma=False)
```
